32 devices in a mesh: tok: 8 (over z, x), feat: 4 (over y, core).
Axes of the slice: x: 2, y: 2, z: 4, core: 2. Of those that a mesh axis runs over, the one named last changes fastest.
Arguments:
- activations: bfloat16 [8192, 28672], P('tok', 'feat'), may hold values from -6 to 6
- out_grads: bfloat16 [8192, 8192], P('tok', 'feat'), may hold values from -6 to 6
- proj_in: bfloat16 [28672, 256], P('feat'), may hold values from -0.03125 to 0.03125
- proj_out: bfloat16 [8192, 256], P('feat'), may hold values from -0.0625 to 0.0625
- left_factor: float32 [256, 256], replicated, may hold values from -0.375 to 0.375
- right_factor: float32 [256, 256], replicated, may hold values from -0.375 to 0.375
- seq_lengths: int32 [64], replicated, may hold values from 1 to 255, as said below
- seq_slots: int32 [64], replicated, may hold values from 0 to 63, each once
- stored_grads: float32 [256, 65536], P('tok', 'feat'), may hold values from -0.375 to 0.375
Outputs:
- scores: float32 [256, 64], P(('tok', 'feat'))
- seq_grads: float32 [64, 65536], P('tok', 'feat')
The draws below stay inside these ranges and needn't reach their ends.
Inputs may be any that keep to these rules, and one draw needn't show every extreme that they name: `seq_lengths`: the lengths sum to 8192. Sequence s starts within tokens s * (128) to (s + 1) * 128 - 1, the first at token 0, so exactly 8 sequences start in the tokens of each index of tok, at most 9 sequences meet them (exactly that many at index 1), and a sequence meets the tokens of at most two indices. The longest is exactly 255. `seq_slots`: every slot is used by exactly one sequence.
All inputs are finite; a program needn't handle non-finite values.
Results may differ from the reference program's by a relative error of at most 0.0003.
Values sent between devices are 32-bit elements; how exact they have to be, the bound alone decides.
A program may use at most 128 MiB of HBM per device.

```python
import jax
import jax.numpy as jnp
from jax import lax

D_IN = 28672
D_OUT = 8192
K = 256
TOK_DEV = 1024
SEQ_DEV = 8
TOKENS = 8192
SEQS = 64
STORE = 256
MOST_LEN = 255


def draw_seq_lengths(key, part):
    spacing = TOK_DEV // SEQ_DEV
    jitter = jax.random.randint(jax.random.fold_in(key, 7), (SEQS,), 0, spacing).astype(jnp.int32)
    jitter = jitter.at[0].set(0)
    jitter = jitter.at[SEQ_DEV - 1].set(0)
    jitter = jitter.at[SEQ_DEV].set(spacing - 1)
    starts = jnp.arange(SEQS, dtype=jnp.int32) * spacing + jitter
    ends = jnp.concatenate([starts[1:], jnp.full((1,), TOKENS, jnp.int32)])
    return (ends - starts).astype(jnp.int32)


def levels(stream_key, dims, cuts, low, largest):
    factor_of, own = 1.0, jax.random.fold_in(stream_key, 6)
    for position, blocks in cuts:
        steps = jnp.exp(jax.random.uniform(jax.random.fold_in(own, position), (blocks,), jnp.float32, low / len(cuts), largest / len(cuts)))
        factor_of = factor_of * jnp.repeat(steps, dims[position] // blocks).reshape([-1 if axis == position else 1 for axis in range(len(dims))])
    return factor_of


def normal_values(stream_key, shape, spread, bound, cuts=(), held_as=jnp.bfloat16):
    level = levels(stream_key, shape, cuts, -0.22, 0.18) if cuts else 1.0
    entries = jax.random.normal(stream_key, shape, jnp.float32) * spread * level
    return jnp.minimum(jnp.maximum(entries, -bound), bound).astype(held_as)


def setup_inputs(seed: int = 0) -> dict:
    splits = jax.random.split(jax.random.key(seed), 10)
    return {
        "activations": normal_values(splits[0], (TOKENS, D_IN), 1.0, 6.0, ((0, 8), (1, 4))),
        "out_grads": normal_values(splits[1], (TOKENS, D_OUT), 1.0, 6.0, ((0, 8), (1, 4))),
        "proj_in": normal_values(splits[2], (D_IN, K), D_IN ** -0.5, 0.03125, ((0, 4),)),
        "proj_out": normal_values(splits[3], (D_OUT, K), D_OUT ** -0.5, 0.0625, ((0, 4),)),
        "left_factor": normal_values(splits[4], (K, K), K ** -0.5, 0.375, (), jnp.float32),
        "right_factor": normal_values(splits[5], (K, K), K ** -0.5, 0.375, (), jnp.float32),
        "seq_lengths": draw_seq_lengths(jax.random.fold_in(splits[9], 71), 0),
        "seq_slots": jax.random.permutation(splits[7], SEQS).astype(jnp.int32),
        "stored_grads": normal_values(splits[8], (STORE, K * K), (16.0 / K), 0.375, ((0, 8), (1, 4)), jnp.float32),
    }


def reference(activations, out_grads, proj_in, proj_out, left_factor, right_factor, seq_lengths, seq_slots, stored_grads):
    in_proj = jnp.dot(activations, proj_in, preferred_element_type=jnp.float32)
    out_proj = jnp.dot(out_grads, proj_out, preferred_element_type=jnp.float32)
    right_side = jnp.dot(in_proj, right_factor, precision=lax.Precision.HIGHEST)
    left_side = jnp.dot(out_proj, left_factor.T, precision=lax.Precision.HIGHEST)
    ends = jnp.cumsum(seq_lengths).astype(jnp.int32)
    starts = (ends - seq_lengths).astype(jnp.int32)

    def one_sequence(pair):
        start, length = pair
        first = jnp.clip(start, 0, TOKENS - MOST_LEN).astype(jnp.int32)
        left_win = lax.dynamic_slice_in_dim(left_side, first, MOST_LEN, 0)
        right_win = lax.dynamic_slice_in_dim(right_side, first, MOST_LEN, 0)
        places = first + jnp.arange(MOST_LEN, dtype=jnp.int32)
        inside = ((places >= start) & (places < start + length)).astype(jnp.float32)
        weights = inside / length.astype(jnp.float32)
        weighted = weights[:, None] * left_win
        return jnp.dot(weighted.T, right_win, precision=lax.Precision.HIGHEST).reshape(K * K)

    per_sequence = lax.map(one_sequence, (starts, seq_lengths))
    seq_grads = jnp.zeros((SEQS, K * K), jnp.float32).at[seq_slots].set(per_sequence)
    scores = jnp.dot(stored_grads, seq_grads.T, precision=lax.Precision.HIGHEST)
    return scores, seq_grads
```

```python
import functools

import jax
import jax.numpy as jnp
from jax import lax
from jax.experimental import pallas as pl
from jax.experimental.pallas import tpu as pltpu
from jax.sharding import PartitionSpec as P

MESH = pl.DeviceIdType.MESH
VMEM = pl.BlockSpec(memory_space=pltpu.VMEM)


def remote(src, dst, send_sem, recv_sem, tok, feat):
    return pltpu.make_async_remote_copy(
        src_ref=src, dst_ref=dst, send_sem=send_sem, recv_sem=recv_sem,
        device_id=(tok, feat), device_id_type=MESH,
    )


def greet(barrier, tok, feat):
    pl.semaphore_signal(barrier, inc=1, device_id=(tok, feat), device_id_type=MESH)


def sum_kernel(chips, rows, *refs):
    ins, outs, first, held, second = refs[0:2], refs[2:4], refs[4:6], refs[6:8], refs[8:10]
    send1, recv1, send2, recv2 = refs[10:14]
    tok, feat = lax.axis_index("tok"), lax.axis_index("feat")
    pair, core = feat // 2, feat % 2
    mate = pair * 2 + (1 - core)
    barrier = pltpu.get_barrier_semaphore()
    greet(barrier, tok, mate)
    for step in range(1, chips):
        greet(barrier, tok, ((pair + step) % chips) * 2 + core)
    pl.semaphore_wait(barrier, chips)

    def block(ref, step, side):
        owner = ((pair + step) % chips) * 2 + side
        return ref.at[pl.ds(pl.multiple_of(owner * rows, rows), rows)]

    order = [(step, k) for step in list(range(1, chips)) + [0] for k in range(2)]
    copies1 = {}
    for step, k in order:
        copies1[step, k] = remote(
            block(ins[k], step, 1 - core), first[k].at[step],
            send1.at[k, step], recv1.at[k, step], tok, mate,
        )
        copies1[step, k].start()
    copies2 = {}
    for step, k in order:
        copies1[step, k].wait_recv()
        held[k][step] = block(ins[k], step, core)[...] + first[k][step]
        if step:
            copies2[step, k] = remote(
                held[k].at[step], second[k].at[step],
                send2.at[k, step], recv2.at[k, step], tok, ((pair + step) % chips) * 2 + core,
            )
            copies2[step, k].start()
    for k in range(2):
        total = held[k][0]
        for step in range(1, chips):
            copies2[step, k].wait_recv()
            total += second[k][step]
        outs[k][...] = total
    for copy in list(copies1.values()) + list(copies2.values()):
        copy.wait_send()


def gather_kernel(feats, groups, local, height, near, offsets, part, out, recv, sends, recvs, usend, urecv):
    tok, feat = lax.axis_index("tok"), lax.axis_index("feat")
    group, half = tok // 2, tok % 2
    count = 2 * feats
    me = half * feats + feat
    barrier = pltpu.get_barrier_semaphore()
    for step in range(1, count):
        peer = (me + step) % count
        greet(barrier, group * 2 + peer // feats, peer % feats)

    @pl.when(group > 0)
    def _():
        greet(barrier, tok - 2, feat)

    @pl.when(group < groups - 1)
    def _():
        greet(barrier, tok + 2, feat)

    ends = (group > 0).astype(jnp.int32) + (group < groups - 1).astype(jnp.int32)
    pl.semaphore_wait(barrier, count - 1 + ends)
    spacing, rows = offsets
    copies = {}
    for step in range(1, count):
        peer = (me + step) % count
        first = pl.multiple_of(((peer % feats) * 2 + peer // feats) * height, height)
        copies[step] = remote(
            part.at[:, pl.ds(first, height), :], recv.at[step],
            sends.at[step], recvs.at[step], group * 2 + peer // feats, peer % feats,
        )
        copies[step].start()
    out[group] = jnp.zeros(out.shape[1:], out.dtype)
    mine = pl.multiple_of((feat * 2 + half) * height, height)
    for step in range(count):
        source = (me + count - step) % count
        base = (source // feats) * local + ((source % feats) * rows) // spacing
        if step:
            copies[step].wait_recv()
        for k in range(near):
            block = recv[step, k] if step else part[k, pl.ds(mine, height), :]
            out[group, base + k] += block

    def up(step):
        at = jnp.maximum(group - step, 0)
        return remote(out.at[at], out.at[at], usend.at[0, step], urecv.at[0, step], tok + 2, feat)

    def down(step):
        at = jnp.minimum(group + step, groups - 1)
        return remote(out.at[at], out.at[at], usend.at[1, step], urecv.at[1, step], tok - 2, feat)

    def each(move, what, when):
        @pl.when(when)
        def _():
            getattr(move, what)()

    for step in range(groups - 1):
        ups = (group - step >= 0) & (group + 1 < groups)
        downs = (group + step < groups) & (group - 1 >= 0)
        each(up(step), "start", ups)
        each(down(step), "start", downs)
        each(up(step), "wait_recv", group - 1 - step >= 0)
        each(down(step), "wait_recv", group + 1 + step < groups)
    for step in range(groups - 1):
        each(up(step), "wait_send", (group - step >= 0) & (group + 1 < groups))
        each(down(step), "wait_send", (group + step < groups) & (group - 1 >= 0))
    for step in range(1, count):
        copies[step].wait_send()


def last_kernel(feats, rows, scores, rows_out, total, recv, sends, recvs, rsend, rrecv):
    tok, feat = lax.axis_index("tok"), lax.axis_index("feat")
    group, half = tok // 2, tok % 2
    count = 2 * feats
    me = half * feats + feat
    barrier = pltpu.get_barrier_semaphore()
    for step in range(1, count):
        peer = (me + step) % count
        greet(barrier, group * 2 + peer // feats, peer % feats)
    pl.semaphore_wait(barrier, count - 1)
    trade = remote(rows, rows_out, rsend, rrecv, group * 2 + 1 - half, feat)
    trade.start()
    copies = {}
    for step in range(1, count):
        peer = (me + step) % count
        copies[step] = remote(
            scores.at[peer], recv.at[step], sends.at[step], recvs.at[step],
            group * 2 + peer // feats, peer % feats,
        )
        copies[step].start()
    summed = scores[me]
    for step in range(1, count):
        copies[step].wait_recv()
        summed += recv[step]
    total[...] = summed
    trade.wait()
    for step in range(1, count):
        copies[step].wait_send()


def body(
    activations,
    out_grads,
    proj_in,
    proj_out,
    left_factor,
    right_factor,
    seq_lengths,
    seq_slots,
    stored_grads,
):
    highest = lax.Precision.HIGHEST
    f32 = jnp.float32
    dma = pltpu.SemaphoreType.DMA
    feats, toks = lax.axis_size("feat"), lax.axis_size("tok")
    chips, groups, count = feats // 2, toks // 2, 2 * feats
    rank = right_factor.shape[0]
    tok_rows = activations.shape[0]
    seq_count = seq_lengths.shape[0]
    local = seq_count // toks
    spacing = tok_rows // local
    rows = tok_rows // feats
    height = rank // count
    near = max(rows // spacing, 1) + 1
    feat, tok = lax.axis_index("feat"), lax.axis_index("tok")
    half = tok % 2
    store_rows, width = stored_grads.shape
    wide = width // 2

    kept = lax.dynamic_slice_in_dim(stored_grads, half * wide, wide, 1)
    given = lax.dynamic_slice_in_dim(stored_grads, (1 - half) * wide, wide, 1)
    taken = lax.ppermute(given, "tok", [(t, t + 1 - 2 * (t % 2)) for t in range(toks)])

    out_part = jnp.dot(out_grads, proj_out, preferred_element_type=f32)
    in_part = jnp.dot(activations, proj_in, preferred_element_type=f32)
    out_total, in_total = pl.pallas_call(
        functools.partial(sum_kernel, chips, rows),
        out_shape=[jax.ShapeDtypeStruct((rows, rank), f32)] * 2,
        in_specs=[VMEM] * 2,
        out_specs=[VMEM] * 2,
        scratch_shapes=[pltpu.VMEM((chips, rows, rank), f32)] * 6 + [dma((2, chips))] * 4,
        compiler_params=pltpu.CompilerParams(collective_id=0, has_side_effects=True),
        name="sum_rows",
    )(out_part, in_part)
    right_side = jnp.dot(in_total, right_factor, precision=highest)
    left_side = jnp.dot(out_total, left_factor.T, precision=highest)

    ends = jnp.cumsum(seq_lengths)
    starts = ends - seq_lengths
    places = tok * tok_rows + feat * rows + jnp.arange(rows, dtype=jnp.int32)
    base = tok * local + (feat * rows) // spacing
    zero = jnp.zeros((1,), jnp.int32)
    near_starts = lax.dynamic_slice_in_dim(jnp.concatenate([zero, starts]), base, near, 0)
    near_ends = lax.dynamic_slice_in_dim(jnp.concatenate([zero, ends]), base, near, 0)
    near_lengths = lax.dynamic_slice_in_dim(jnp.concatenate([zero + 1, seq_lengths]), base, near, 0)
    inside = (
        (places[:, None] >= near_starts[None, :]) & (places[:, None] < near_ends[None, :])
    ).astype(f32)
    weights = inside / near_lengths.astype(f32)[None, :]
    spread = jnp.concatenate([weights[:, k : k + 1] * left_side for k in range(near)], axis=1)
    part = lax.dot_general(spread, right_side, (((0,), (0,)), ((), ())), precision=highest)

    blocks = 2 * local + 1
    gathered = pl.pallas_call(
        functools.partial(gather_kernel, feats, groups, local, height, near, (spacing, rows)),
        out_shape=jax.ShapeDtypeStruct((groups, blocks, height, rank), f32),
        in_specs=[VMEM],
        out_specs=VMEM,
        scratch_shapes=[
            pltpu.VMEM((count, near, height, rank), f32),
            dma((count,)),
            dma((count,)),
            dma((2, max(groups - 1, 1))),
            dma((2, max(groups - 1, 1))),
        ],
        compiler_params=pltpu.CompilerParams(collective_id=1, has_side_effects=True),
        name="gather_rows",
    )(part.reshape(near, rank, rank))
    flat = gathered.reshape(groups * blocks, wide)

    spots = jnp.arange(groups * blocks, dtype=jnp.int32)
    numbers = (spots // blocks) * (2 * local) + spots % blocks - 1
    slot_of = jnp.where(numbers >= 0, jnp.take(seq_slots, jnp.maximum(numbers, 0)), -1)
    chosen = (jnp.arange(seq_count, dtype=jnp.int32)[:, None] == slot_of[None, :]).astype(f32)
    all_grads = jnp.dot(chosen, flat, precision=highest)
    own = lax.dynamic_slice_in_dim(all_grads, tok * local, local, 0)
    other = lax.dynamic_slice_in_dim(all_grads, (tok + 1 - 2 * half) * local, local, 0)
    products = [
        lax.dot_general(rows_, all_grads, (((1,), (1,)), ((), ())), precision=highest)
        for rows_ in (kept, taken)
    ]
    is_low = half == 0
    low = jnp.where(is_low, products[0], products[1])
    high = jnp.where(is_low, products[1], products[0])
    pad = -seq_count % 128
    scores_part = jnp.pad(jnp.concatenate([low, high], axis=0), ((0, 0), (0, pad)))
    score_rows = store_rows // feats
    scores_part = scores_part.reshape(count, score_rows, seq_count + pad)
    traded, scores = pl.pallas_call(
        functools.partial(last_kernel, feats),
        out_shape=[
            jax.ShapeDtypeStruct((local, wide), f32),
            jax.ShapeDtypeStruct((score_rows, seq_count + pad), f32),
        ],
        in_specs=[VMEM] * 2,
        out_specs=[VMEM] * 2,
        scratch_shapes=[
            pltpu.VMEM((count, score_rows, seq_count + pad), f32),
            dma((count,)),
            dma((count,)),
            dma,
            dma,
        ],
        compiler_params=pltpu.CompilerParams(collective_id=2, has_side_effects=True),
        name="last_rows",
    )(other, scores_part)
    own_rows = jnp.concatenate(
        [jnp.where(is_low, own, traded), jnp.where(is_low, traded, own)], axis=1
    )
    return scores[:, :seq_count], own_rows


def solution(mesh):
    placed = (
        P("tok", "feat"),
        P("tok", "feat"),
        P("feat", None),
        P("feat", None),
        P(),
        P(),
        P(),
        P(),
        P("tok", "feat"),
    )
    return jax.shard_map(
        body,
        mesh=mesh,
        in_specs=placed,
        out_specs=(P(("tok", "feat"), None), P("tok", "feat")),
        check_vma=False,
    )
```

```python
import functools

import jax
import jax.numpy as jnp
from jax import lax
from jax.experimental import pallas as pl
from jax.experimental.pallas import tpu as pltpu
from jax.sharding import PartitionSpec as P

MESH = pl.DeviceIdType.MESH
VMEM = pl.BlockSpec(memory_space=pltpu.VMEM)


def remote(src, dst, send_sem, recv_sem, tok, feat):
    return pltpu.make_async_remote_copy(
        src_ref=src, dst_ref=dst, send_sem=send_sem, recv_sem=recv_sem,
        device_id=(tok, feat), device_id_type=MESH,
    )


def greet(barrier, tok, feat):
    pl.semaphore_signal(barrier, inc=1, device_id=(tok, feat), device_id_type=MESH)


def sum_kernel(chips, rows, *refs):
    ins, outs, first, held, second = refs[0:2], refs[2:4], refs[4:6], refs[6:8], refs[8:10]
    send1, recv1, send2, recv2 = refs[10:14]
    tok, feat = lax.axis_index("tok"), lax.axis_index("feat")
    pair, core = feat // 2, feat % 2
    mate = pair * 2 + (1 - core)
    barrier = pltpu.get_barrier_semaphore()
    greet(barrier, tok, mate)
    for step in range(1, chips):
        greet(barrier, tok, ((pair + step) % chips) * 2 + core)
    pl.semaphore_wait(barrier, chips)

    def block(ref, step, side):
        owner = ((pair + step) % chips) * 2 + side
        return ref.at[pl.ds(pl.multiple_of(owner * rows, rows), rows)]

    order = [(step, k) for step in list(range(1, chips)) + [0] for k in range(2)]
    copies1 = {}
    for step, k in order:
        copies1[step, k] = remote(
            block(ins[k], step, 1 - core), first[k].at[step],
            send1.at[k, step], recv1.at[k, step], tok, mate,
        )
        copies1[step, k].start()
    copies2 = {}
    for step, k in order:
        copies1[step, k].wait_recv()
        held[k][step] = block(ins[k], step, core)[...] + first[k][step]
        if step:
            copies2[step, k] = remote(
                held[k].at[step], second[k].at[step],
                send2.at[k, step], recv2.at[k, step], tok, ((pair + step) % chips) * 2 + core,
            )
            copies2[step, k].start()
    for k in range(2):
        total = held[k][0]
        for step in range(1, chips):
            copies2[step, k].wait_recv()
            total += second[k][step]
        outs[k][...] = total
    for copy in list(copies1.values()) + list(copies2.values()):
        copy.wait_send()


def grads_kernel(sizes, part, chosen, *refs):
    feats, group_toks, groups, local, rows, spacing, pieces = sizes
    stored = refs[:group_toks]
    total, out = refs[group_toks : group_toks + 2]
    recv, grads, heads, picked, scored, landed = refs[group_toks + 2 : group_toks + 8]
    sends, recvs, gsend, grecv, hsend, hrecv, psend, precv, ssend, srecv = refs[group_toks + 8 :]
    highest = lax.Precision.HIGHEST
    near, count, height, rank = part.shape
    held = group_toks * local
    tall = height // pieces
    tok, feat = lax.axis_index("tok"), lax.axis_index("feat")
    group, spot = tok // group_toks, tok % group_toks
    me = spot * feats + feat

    def place(step):
        peer = (me + step) % count
        return peer // feats, peer % feats

    barrier = pltpu.get_barrier_semaphore()
    for step in range(1, count):
        peer_spot, peer_feat = place(step)
        greet(barrier, group * group_toks + peer_spot, peer_feat)

    @pl.when(group > 0)
    def _():
        greet(barrier, tok - group_toks, feat)

    @pl.when(group < groups - 1)
    def _():
        greet(barrier, tok + group_toks, feat)

    ends = (group > 0).astype(jnp.int32) + (group < groups - 1).astype(jnp.int32)
    pl.semaphore_wait(barrier, count - 1 + ends)

    copies = {}
    for piece in range(pieces):
        lines = pl.ds(piece * tall, tall)
        for step in range(1, count):
            peer_spot, peer_feat = place(step)
            copies[piece, step] = remote(
                part.at[:, peer_feat * group_toks + peer_spot, lines, :],
                recv.at[step, :, lines, :],
                sends.at[piece, step], recvs.at[piece, step],
                group * group_toks + peer_spot, peer_feat,
            )
            copies[piece, step].start()
    recv[0] = part[:, feat * group_toks + spot]

    terms = {}
    for source in range(count):
        base = (source // feats) * local + ((source % feats) * rows) // spacing
        for k in range(near):
            terms.setdefault(base + k, []).append((source, k))

    def block(at, piece):
        return grads.at[
            pl.ds(piece * tall, tall), pl.ds(pl.multiple_of(at * held, held), held), :
        ]

    def move(way, step, piece):
        at = jnp.clip(group - step if way == 0 else group + step, 0, groups - 1)
        to = tok + group_toks if way == 0 else tok - group_toks
        head = heads.at[at, pl.ds(piece * tall, tall), :]
        index = way, step, piece
        return (
            remote(block(at, piece), block(at, piece), gsend.at[index], grecv.at[index], to, feat),
            remote(head, head, hsend.at[index], hrecv.at[index], to, feat),
        )

    def each(way, step, piece, what, when):
        @pl.when(when)
        def _():
            for copy in move(way, step, piece):
                getattr(copy, what)()

    def sending(way, step):
        if way == 0:
            return (group - step >= 0) & (group + 1 < groups)
        return (group + step < groups) & (group - 1 >= 0)

    def taking(way, step):
        return group - 1 - step >= 0 if way == 0 else group + 1 + step < groups

    for piece in range(pieces):
        lines = pl.ds(piece * tall, tall)
        for step in range(1, count):
            copies[piece, step].wait_recv()
        for row in range(held + 1):
            value = None
            for source, k in terms.get(row, []):
                term = recv[(me + count - source) % count, k, lines, :]
                value = term if value is None else value + term
            if row == 0:
                heads[group, lines, :] = value
            else:
                block(group, piece)[:, row - 1, :] = value
        for way in range(2):
            if groups > 1:
                each(way, 0, piece, "start", sending(way, 0))
    for step in range(groups - 1):
        for piece in range(pieces):
            for way in range(2):
                each(way, step, piece, "wait_recv", taking(way, step))
                if step + 1 < groups - 1:
                    each(way, step + 1, piece, "start", sending(way, step + 1))
    for step in range(groups - 1):
        for piece in range(pieces):
            for way in range(2):
                each(way, step, piece, "wait_send", sending(way, step))

    for at in range(1, groups):
        grads[:, at * held - 1, :] += heads[at]
    pick = chosen[...]
    for line in range(height):
        lane = pl.ds(line * rank, rank)
        taken = jnp.dot(pick, grads[line], precision=highest, preferred_element_type=jnp.float32)
        for q in range(group_toks):
            picked[q, :, lane] = taken[q * local : (q + 1) * local]
    wide = height * rank
    mine = pl.ds(pl.multiple_of(spot * wide, wide), wide)
    trades = []
    for step in range(1, group_toks):
        to = (spot + step) % group_toks
        trades.append(remote(
            picked.at[to], out.at[:, mine], psend.at[step], precv.at[step],
            group * group_toks + to, feat,
        ))
        trades[-1].start()
    out[:, mine] = picked[spot]

    score = jnp.zeros((group_toks * stored[0].shape[0], grads.shape[1]), jnp.float32)
    for line in range(height):
        lane = pl.ds(line * rank, rank)
        kept = jnp.concatenate([ref[:, lane] for ref in stored], axis=0)
        score += lax.dot_general(
            kept, grads[line], (((1,), (1,)), ((), ())),
            precision=highest, preferred_element_type=jnp.float32,
        )
    scored[...] = jnp.zeros_like(scored)
    few = total.shape[0]
    for step in range(group_toks):
        for f in range(feats):
            first = (step * feats + f) * few
            scored[step, f, :, : score.shape[1]] = score[first : first + few]
    parts = []
    for step in range(group_toks):
        for turn in range(feats):
            if step or turn:
                to = (feat + turn) % feats
                parts.append(remote(
                    scored.at[step, to], landed.at[step, turn],
                    ssend.at[step, turn], srecv.at[step, turn],
                    group * group_toks + (spot + group_toks - step) % group_toks, to,
                ))
                parts[-1].start()
    summed = scored[0, feat]
    for number, copy in enumerate(parts, 1):
        copy.wait_recv()
        summed += landed[number // feats, number % feats]
    total[...] = summed
    for copy in trades:
        copy.wait_recv()
    for copy in trades + parts + list(copies.values()):
        copy.wait_send()


def body(
    activations,
    out_grads,
    proj_in,
    proj_out,
    left_factor,
    right_factor,
    seq_lengths,
    seq_slots,
    stored_grads,
):
    highest = lax.Precision.HIGHEST
    f32 = jnp.float32
    dma = pltpu.SemaphoreType.DMA
    feats, toks = lax.axis_size("feat"), lax.axis_size("tok")
    group_toks = 4 if toks % 4 == 0 else 1
    chips, groups, count = feats // 2, toks // group_toks, group_toks * feats
    rank = right_factor.shape[0]
    tok_rows = activations.shape[0]
    seq_count = seq_lengths.shape[0]
    local = seq_count // toks
    spacing = tok_rows // local
    rows = tok_rows // feats
    height = rank // count
    near = max(rows // spacing, 1) + 1
    feat, tok = lax.axis_index("feat"), lax.axis_index("tok")
    spot = tok % group_toks
    store_rows, width = stored_grads.shape
    wide = width // group_toks

    stored = []
    for step in range(group_toks):
        to = (spot + step) % group_toks
        given = lax.dynamic_slice_in_dim(stored_grads, to * wide, wide, 1)
        pairs = [(t, t - t % group_toks + (t + step) % group_toks) for t in range(toks)]
        stored.append(lax.ppermute(given, "tok", pairs) if step else given)

    out_part = jnp.dot(out_grads, proj_out, preferred_element_type=f32)
    in_part = jnp.dot(activations, proj_in, preferred_element_type=f32)
    out_total, in_total = pl.pallas_call(
        functools.partial(sum_kernel, chips, rows),
        out_shape=[jax.ShapeDtypeStruct((rows, rank), f32)] * 2,
        in_specs=[VMEM] * 2,
        out_specs=[VMEM] * 2,
        scratch_shapes=[pltpu.VMEM((chips, rows, rank), f32)] * 6 + [dma((2, chips))] * 4,
        compiler_params=pltpu.CompilerParams(collective_id=0, has_side_effects=True),
        name="sum_rows",
    )(out_part, in_part)
    right_side = jnp.dot(in_total, right_factor, precision=highest)
    left_side = jnp.dot(out_total, left_factor.T, precision=highest)

    places = tok * tok_rows + feat * rows + jnp.arange(rows, dtype=jnp.int32)
    numbers = jnp.arange(seq_count, dtype=jnp.int32)
    close = tok * local + (feat * rows) // spacing - 1 + jnp.arange(near, dtype=jnp.int32)
    starts = jnp.sum(jnp.where(numbers[None, :] < close[:, None], seq_lengths[None, :], 0), axis=1)
    sizes = jnp.sum(jnp.where(numbers[None, :] == close[:, None], seq_lengths[None, :], 0), axis=1)
    inside = (places[:, None] >= starts[None, :]) & (places[:, None] < (starts + sizes)[None, :])
    weights = inside.astype(f32) / jnp.maximum(sizes, 1).astype(f32)[None, :]
    spread = jnp.concatenate([weights[:, k : k + 1] * left_side for k in range(near)], axis=1)
    part = lax.dot_general(spread, right_side, (((0,), (0,)), ((), ())), precision=highest)

    held = group_toks * local
    slots = (tok // group_toks) * held + jnp.arange(held, dtype=jnp.int32)
    chosen = (slots[:, None] == seq_slots[None, :]).astype(f32)
    score_rows = store_rows // feats
    lanes = seq_count + -seq_count % 128
    pieces = 2 if height % 16 == 0 else 1
    hops = max(groups - 1, 1)
    sizes_ = (feats, group_toks, groups, local, rows, spacing, pieces)
    scores, own_rows = pl.pallas_call(
        functools.partial(grads_kernel, sizes_),
        out_shape=[
            jax.ShapeDtypeStruct((score_rows, lanes), f32),
            jax.ShapeDtypeStruct((local, width), f32),
        ],
        in_specs=[VMEM] * (2 + group_toks),
        out_specs=[VMEM] * 2,
        scratch_shapes=[
            pltpu.VMEM((count, near, height, rank), f32),
            pltpu.VMEM((height, seq_count, rank), f32),
            pltpu.VMEM((groups, height, rank), f32),
            pltpu.VMEM((group_toks, local, wide), f32),
            pltpu.VMEM((group_toks, feats, score_rows, lanes), f32),
            pltpu.VMEM((group_toks, feats, score_rows, lanes), f32),
        ]
        + [dma((pieces, count))] * 2
        + [dma((2, hops, pieces))] * 4
        + [dma((group_toks,))] * 2
        + [dma((group_toks, feats))] * 2,
        compiler_params=pltpu.CompilerParams(collective_id=1, has_side_effects=True),
        name="grads",
    )(part.reshape(near, count, height, rank), chosen, *stored)
    slot_of = (seq_slots[:, None] == numbers[None, :]).astype(f32)
    return jnp.dot(scores[:, :seq_count], slot_of, precision=highest), own_rows


def solution(mesh):
    placed = (
        P("tok", "feat"),
        P("tok", "feat"),
        P("feat", None),
        P("feat", None),
        P(),
        P(),
        P(),
        P(),
        P("tok", "feat"),
    )
    return jax.shard_map(
        body,
        mesh=mesh,
        in_specs=placed,
        out_specs=(P(("tok", "feat"), None), P("tok", "feat")),
        check_vma=False,
    )
```

```python
import functools

import jax
import jax.numpy as jnp
from jax import lax
from jax.experimental import pallas as pl
from jax.experimental.pallas import tpu as pltpu
from jax.sharding import PartitionSpec as P

MESH = pl.DeviceIdType.MESH
VMEM = pl.BlockSpec(memory_space=pltpu.VMEM)


def remote(src, dst, send_sem, recv_sem, tok, feat):
    return pltpu.make_async_remote_copy(
        src_ref=src, dst_ref=dst, send_sem=send_sem, recv_sem=recv_sem,
        device_id=(tok, feat), device_id_type=MESH,
    )


def greet(barrier, tok, feat):
    pl.semaphore_signal(barrier, inc=1, device_id=(tok, feat), device_id_type=MESH)


def project_kernel(sizes, *refs):
    chips, rows, group_toks, early = sizes
    rows_in, mats_in, stored = refs[0:2], refs[2:4], refs[4]
    outs, traded = refs[5:7], refs[7 : 7 + early]
    refs = refs[7 + early :]
    lhs, rhs, parts, first, held, second = (refs[2 * n : 2 * n + 2] for n in range(6))
    load, send1, recv1, send2, recv2, tsend, trecv = refs[12:]
    tok, feat = lax.axis_index("tok"), lax.axis_index("feat")
    spot = tok % group_toks
    pair, core = feat // 2, feat % 2
    mate = pair * 2 + (1 - core)
    both = 2 * rows
    order = list(range(1, chips)) + [0]

    def lines(step):
        return pl.ds(pl.multiple_of(((pair + step) % chips) * both, both), both)

    loads = {}
    for step in order:
        for k in range(2):
            if step == order[0]:
                loads[k] = pltpu.make_async_copy(mats_in[k], rhs[k], load.at[k, chips])
                loads[k].start()
            loads[k, step] = pltpu.make_async_copy(
                rows_in[k].at[lines(step)], lhs[k].at[step], load.at[k, step]
            )
            loads[k, step].start()

    barrier = pltpu.get_barrier_semaphore()
    greet(barrier, tok, mate)
    for step in range(1, chips):
        greet(barrier, tok, ((pair + step) % chips) * 2 + core)
    for step in range(1, group_toks):
        greet(barrier, tok - spot + (spot + step) % group_toks, feat)
    pl.semaphore_wait(barrier, chips + group_toks - 1)

    wide = traded[0].shape[1]
    trades = []
    for step in range(1, early + 1):
        to = (spot + step) % group_toks
        trades.append(remote(
            stored.at[:, pl.ds(pl.multiple_of(to * wide, wide), wide)], traded[step - 1],
            tsend.at[step - 1], trecv.at[step - 1], tok - spot + to, feat,
        ))
        trades[-1].start()

    copies1, copies2 = {}, {}

    def project(k, step, low, high):
        return jnp.dot(
            lhs[k][step, :, low:high], rhs[k][low:high, :], preferred_element_type=jnp.float32
        )

    def to_mate(k, step):
        copies1[k, step] = remote(
            parts[k].at[step, pl.ds(pl.multiple_of((1 - core) * rows, rows), rows)],
            first[k].at[step], send1.at[k, step], recv1.at[k, step], tok, mate,
        )
        copies1[k, step].start()

    def onward(k, step):
        copies1[k, step].wait_recv()
        own = parts[k][step, pl.ds(pl.multiple_of(core * rows, rows), rows), :]
        held[k][step] = own + first[k][step]
        if step:
            copies2[k, step] = remote(
                held[k].at[step], second[k].at[step], send2.at[k, step], recv2.at[k, step],
                tok, ((pair + step) % chips) * 2 + core,
            )
            copies2[k, step].start()

    waiting = []
    for number, step in enumerate(order):
        for k in range(2):
            if number == 0:
                loads[k].wait()
            loads[k, step].wait()
            depth = lhs[k].shape[2]
            cut = depth // 2 if k else depth
            parts[k][step] = project(k, step, 0, cut)
            for item in waiting:
                onward(*item)
            waiting = []
            if cut < depth:
                parts[k][step] += project(k, step, cut, depth)
            to_mate(k, step)
            waiting = [(k, step)]
    for item in waiting:
        onward(*item)
    for k in range(2):
        total = held[k][0]
        for step in range(1, chips):
            copies2[k, step].wait_recv()
            total += second[k][step]
        outs[k][...] = total
    for copy in trades:
        copy.wait_recv()
    for copy in trades + list(copies1.values()) + list(copies2.values()):
        copy.wait_send()


def grads_kernel(sizes, part, chosen, slot_of, stored_rows, *refs):
    feats, group_toks, groups, local, rows, spacing, pieces, early = sizes
    total, out = refs[early : early + 2]
    recv, grads, heads, picked, scored, landed, late = refs[early + 2 : early + 9]
    sends, recvs, gsend, grecv, hsend, hrecv, psend, precv, ssend, srecv, lsend, lrecv = refs[
        early + 9 :
    ]
    highest = lax.Precision.HIGHEST
    near, count, height, rank = part.shape
    held = group_toks * local
    tall = height // pieces
    tok, feat = lax.axis_index("tok"), lax.axis_index("feat")
    group, spot = tok // group_toks, tok % group_toks
    me = spot * feats + feat

    def place(step):
        peer = (me + step) % count
        return peer // feats, peer % feats

    barrier = pltpu.get_barrier_semaphore()
    for step in range(1, count):
        peer_spot, peer_feat = place(step)
        greet(barrier, group * group_toks + peer_spot, peer_feat)

    @pl.when(group > 0)
    def _():
        greet(barrier, tok - group_toks, feat)

    @pl.when(group < groups - 1)
    def _():
        greet(barrier, tok + group_toks, feat)

    ends = (group > 0).astype(jnp.int32) + (group < groups - 1).astype(jnp.int32)
    pl.semaphore_wait(barrier, count - 1 + ends)

    copies = {}
    for piece in range(pieces):
        lines = pl.ds(piece * tall, tall)
        for step in range(1, count):
            peer_spot, peer_feat = place(step)
            copies[piece, step] = remote(
                part.at[:, peer_feat * group_toks + peer_spot, lines, :],
                recv.at[step, :, lines, :],
                sends.at[piece, step], recvs.at[piece, step],
                group * group_toks + peer_spot, peer_feat,
            )
            copies[piece, step].start()
    recv[0] = part[:, feat * group_toks + spot]
    width = late.shape[2]
    kept = pltpu.make_async_copy(
        stored_rows.at[:, pl.ds(pl.multiple_of(spot * width, width), width)], late.at[0], lsend.at[0]
    )
    kept.start()
    trades = []
    for step in range(early + 1, group_toks):
        to = (spot + step) % group_toks
        trades.append(remote(
            stored_rows.at[:, pl.ds(pl.multiple_of(to * width, width), width)],
            late.at[step - early], lsend.at[step - early], lrecv.at[step - early],
            group * group_toks + to, feat,
        ))
        trades[-1].start()
    stored = [late.at[0], *refs[:early]] + [
        late.at[step - early] for step in range(early + 1, group_toks)
    ]

    terms = {}
    for source in range(count):
        base = (source // feats) * local + ((source % feats) * rows) // spacing
        for k in range(near):
            terms.setdefault(base + k, []).append((source, k))

    def block(at, piece):
        return grads.at[
            pl.ds(piece * tall, tall), pl.ds(pl.multiple_of(at * held, held), held), :
        ]

    def move(way, step, piece):
        at = jnp.clip(group - step if way == 0 else group + step, 0, groups - 1)
        to = tok + group_toks if way == 0 else tok - group_toks
        head = heads.at[at, pl.ds(piece * tall, tall), :]
        index = way, step, piece
        return (
            remote(block(at, piece), block(at, piece), gsend.at[index], grecv.at[index], to, feat),
            remote(head, head, hsend.at[index], hrecv.at[index], to, feat),
        )

    def each(way, step, piece, what, when):
        @pl.when(when)
        def _():
            for copy in move(way, step, piece):
                getattr(copy, what)()

    def sending(way, step):
        if way == 0:
            return (group - step >= 0) & (group + 1 < groups)
        return (group + step < groups) & (group - 1 >= 0)

    def taking(way, step):
        return group - 1 - step >= 0 if way == 0 else group + 1 + step < groups

    for piece in range(pieces):
        lines = pl.ds(piece * tall, tall)
        for step in range(1, count):
            copies[piece, step].wait_recv()
        for row in range(held + 1):
            value = None
            for source, k in terms.get(row, []):
                term = recv[(me + count - source) % count, k, lines, :]
                value = term if value is None else value + term
            if row == 0:
                heads[group, lines, :] = value
            else:
                block(group, piece)[:, row - 1, :] = value
        for way in range(2):
            if groups > 1:
                each(way, 0, piece, "start", sending(way, 0))
    for step in range(groups - 1):
        for piece in range(pieces):
            for way in range(2):
                each(way, step, piece, "wait_recv", taking(way, step))
                if step + 1 < groups - 1:
                    each(way, step + 1, piece, "start", sending(way, step + 1))
    for step in range(groups - 1):
        for piece in range(pieces):
            for way in range(2):
                each(way, step, piece, "wait_send", sending(way, step))

    for at in range(1, groups):
        grads[:, at * held - 1, :] += heads[at]
    pick = chosen[...]
    for line in range(height):
        lane = pl.ds(line * rank, rank)
        taken = jnp.dot(pick, grads[line], precision=highest, preferred_element_type=jnp.float32)
        for q in range(group_toks):
            picked[q, :, lane] = taken[q * local : (q + 1) * local]
    wide = height * rank
    mine = pl.ds(pl.multiple_of(spot * wide, wide), wide)
    for step in range(1, group_toks):
        to = (spot + step) % group_toks
        trades.append(remote(
            picked.at[to], out.at[:, mine], psend.at[step], precv.at[step],
            group * group_toks + to, feat,
        ))
        trades[-1].start()
    out[:, mine] = picked[spot]

    kept.wait()
    for copy in trades[: group_toks - 1 - early]:
        copy.wait_recv()
    score = jnp.zeros((group_toks * late.shape[1], grads.shape[1]), jnp.float32)
    for line in range(height):
        lane = pl.ds(line * rank, rank)
        lanes = jnp.concatenate([ref[:, lane] for ref in stored], axis=0)
        score += lax.dot_general(
            lanes, grads[line], (((1,), (1,)), ((), ())),
            precision=highest, preferred_element_type=jnp.float32,
        )
    scored[...] = jnp.zeros_like(scored)
    few = scored.shape[2]
    for step in range(group_toks):
        for f in range(feats):
            first = (step * feats + f) * few
            scored[step, f, :, : score.shape[1]] = score[first : first + few]
    parts = []
    for step in range(group_toks):
        for turn in range(feats):
            if step or turn:
                to = (feat + turn) % feats
                parts.append(remote(
                    scored.at[step, to], landed.at[step, turn],
                    ssend.at[step, turn], srecv.at[step, turn],
                    group * group_toks + (spot + group_toks - step) % group_toks, to,
                ))
                parts[-1].start()
    summed = scored[0, feat]
    for number, copy in enumerate(parts, 1):
        copy.wait_recv()
        summed += landed[number // feats, number % feats]
    total[...] = jnp.dot(
        summed[:, : score.shape[1]], slot_of[...], precision=highest,
        preferred_element_type=jnp.float32,
    )
    for copy in trades[group_toks - 1 - early :]:
        copy.wait_recv()
    for copy in trades + parts + list(copies.values()):
        copy.wait_send()


def body(
    activations,
    out_grads,
    proj_in,
    proj_out,
    left_factor,
    right_factor,
    seq_lengths,
    seq_slots,
    stored_grads,
):
    highest = lax.Precision.HIGHEST
    f32 = jnp.float32
    dma = pltpu.SemaphoreType.DMA
    feats, toks = lax.axis_size("feat"), lax.axis_size("tok")
    group_toks = 4 if toks % 4 == 0 else 1
    chips, groups, count = feats // 2, toks // group_toks, group_toks * feats
    rank = right_factor.shape[0]
    tok_rows = activations.shape[0]
    seq_count = seq_lengths.shape[0]
    local = seq_count // toks
    spacing = tok_rows // local
    rows = tok_rows // feats
    height = rank // count
    near = max(rows // spacing, 1) + 1
    feat, tok = lax.axis_index("feat"), lax.axis_index("tok")
    spot = tok % group_toks
    store_rows, width = stored_grads.shape
    wide = width // group_toks

    early = max(group_toks - 2, 1)
    any_space = pl.BlockSpec(memory_space=pl.ANY)
    lefts, mats = (out_grads, activations), (proj_out, proj_in)
    pair_rows = pltpu.VMEM((chips, rows, rank), f32)
    out_total, in_total, *traded = pl.pallas_call(
        functools.partial(project_kernel, (chips, rows, group_toks, early)),
        out_shape=[jax.ShapeDtypeStruct((rows, rank), f32)] * 2
        + [jax.ShapeDtypeStruct((store_rows, wide), f32)] * early,
        in_specs=[any_space] * 5,
        out_specs=[VMEM] * (2 + early),
        scratch_shapes=[pltpu.VMEM((chips, 2 * rows, m.shape[1]), m.dtype) for m in lefts]
        + [pltpu.VMEM(m.shape, m.dtype) for m in mats]
        + [pltpu.VMEM((chips, 2 * rows, rank), f32)] * 2
        + [pair_rows] * 6
        + [dma((2, chips + 1))]
        + [dma((2, chips))] * 4
        + [dma((early,))] * 2,
        compiler_params=pltpu.CompilerParams(
            collective_id=0, has_side_effects=True, vmem_limit_bytes=60 << 20
        ),
        name="project",
    )(*lefts, *mats, stored_grads)
    right_side = jnp.dot(in_total, right_factor, precision=highest)
    left_side = jnp.dot(out_total, left_factor.T, precision=highest)

    places = tok * tok_rows + feat * rows + jnp.arange(rows, dtype=jnp.int32)
    numbers = jnp.arange(seq_count, dtype=jnp.int32)
    close = tok * local + (feat * rows) // spacing - 1 + jnp.arange(near, dtype=jnp.int32)
    starts = jnp.sum(jnp.where(numbers[None, :] < close[:, None], seq_lengths[None, :], 0), axis=1)
    sizes = jnp.sum(jnp.where(numbers[None, :] == close[:, None], seq_lengths[None, :], 0), axis=1)
    inside = (places[:, None] >= starts[None, :]) & (places[:, None] < (starts + sizes)[None, :])
    weights = inside.astype(f32) / jnp.maximum(sizes, 1).astype(f32)[None, :]
    spread = jnp.concatenate([weights[:, k : k + 1] * left_side for k in range(near)], axis=1)
    part = lax.dot_general(spread, right_side, (((0,), (0,)), ((), ())), precision=highest)

    held = group_toks * local
    slots = (tok // group_toks) * held + jnp.arange(held, dtype=jnp.int32)
    chosen = (slots[:, None] == seq_slots[None, :]).astype(f32)
    score_rows = store_rows // feats
    lanes = seq_count + -seq_count % 128
    pieces = 2 if height % 16 == 0 else 1
    hops = max(groups - 1, 1)
    sizes_ = (feats, group_toks, groups, local, rows, spacing, pieces, early)
    slot_of = (seq_slots[:, None] == numbers[None, :]).astype(f32)
    scores, own_rows = pl.pallas_call(
        functools.partial(grads_kernel, sizes_),
        out_shape=[
            jax.ShapeDtypeStruct((score_rows, seq_count), f32),
            jax.ShapeDtypeStruct((local, width), f32),
        ],
        in_specs=[VMEM] * 3 + [any_space] + [VMEM] * early,
        out_specs=[VMEM] * 2,
        scratch_shapes=[
            pltpu.VMEM((count, near, height, rank), f32),
            pltpu.VMEM((height, seq_count, rank), f32),
            pltpu.VMEM((groups, height, rank), f32),
            pltpu.VMEM((group_toks, local, wide), f32),
            pltpu.VMEM((group_toks, feats, score_rows, lanes), f32),
            pltpu.VMEM((group_toks, feats, score_rows, lanes), f32),
            pltpu.VMEM((group_toks - early, store_rows, wide), f32),
        ]
        + [dma((pieces, count))] * 2
        + [dma((2, hops, pieces))] * 4
        + [dma((group_toks,))] * 2
        + [dma((group_toks, feats))] * 2
        + [dma((group_toks - early,))] * 2,
        compiler_params=pltpu.CompilerParams(collective_id=1, has_side_effects=True),
        name="grads",
    )(part.reshape(near, count, height, rank), chosen, slot_of, stored_grads, *traded)
    return scores, own_rows


def solution(mesh):
    placed = (
        P("tok", "feat"),
        P("tok", "feat"),
        P("feat", None),
        P("feat", None),
        P(),
        P(),
        P(),
        P(),
        P("tok", "feat"),
    )
    return jax.shard_map(
        body,
        mesh=mesh,
        in_specs=placed,
        out_specs=(P(("tok", "feat"), None), P("tok", "feat")),
        check_vma=False,
    )
```

```python
import functools

import jax
import jax.numpy as jnp
from jax import lax
from jax.experimental import pallas as pl
from jax.experimental.pallas import tpu as pltpu
from jax.sharding import PartitionSpec as P

MESH = pl.DeviceIdType.MESH
VMEM = pl.BlockSpec(memory_space=pltpu.VMEM)


def remote(src, dst, send_sem, recv_sem, tok, feat):
    return pltpu.make_async_remote_copy(
        src_ref=src, dst_ref=dst, send_sem=send_sem, recv_sem=recv_sem,
        device_id=(tok, feat), device_id_type=MESH,
    )


def greet(barrier, tok, feat):
    pl.semaphore_signal(barrier, inc=1, device_id=(tok, feat), device_id_type=MESH)


def project_kernel(sizes, *refs):
    chips, rows, group_toks, early = sizes
    rows_in, mats_in, stored = refs[0:2], refs[2:4], refs[4]
    outs, traded = refs[5:7], refs[7 : 7 + early]
    refs = refs[7 + early :]
    lhs, rhs, parts, first, held, second = (refs[2 * n : 2 * n + 2] for n in range(6))
    load, send1, recv1, send2, recv2, tsend, trecv = refs[12:]
    tok, feat = lax.axis_index("tok"), lax.axis_index("feat")
    spot = tok % group_toks
    pair, core = feat // 2, feat % 2
    mate = pair * 2 + (1 - core)
    both = 2 * rows
    order = list(range(1, chips)) + [0]

    def lines(step):
        return pl.ds(pl.multiple_of(((pair + step) % chips) * both, both), both)

    loads = {}
    for step in order:
        for k in range(2):
            if step == order[0]:
                loads[k] = pltpu.make_async_copy(mats_in[k], rhs[k], load.at[k, chips])
                loads[k].start()
            loads[k, step] = pltpu.make_async_copy(
                rows_in[k].at[lines(step)], lhs[k].at[step], load.at[k, step]
            )
            loads[k, step].start()

    barrier = pltpu.get_barrier_semaphore()
    greet(barrier, tok, mate)
    for step in range(1, chips):
        greet(barrier, tok, ((pair + step) % chips) * 2 + core)
    for step in range(1, group_toks):
        greet(barrier, tok - spot + (spot + step) % group_toks, feat)
    pl.semaphore_wait(barrier, chips + group_toks - 1)

    wide = traded[0].shape[1]
    trades = []
    for step in range(1, early + 1):
        to = (spot + step) % group_toks
        trades.append(remote(
            stored.at[:, pl.ds(pl.multiple_of(to * wide, wide), wide)], traded[step - 1],
            tsend.at[step - 1], trecv.at[step - 1], tok - spot + to, feat,
        ))
        trades[-1].start()

    copies1, copies2 = {}, {}

    def project(k, step, low, high):
        return jnp.dot(
            lhs[k][step, :, low:high], rhs[k][low:high, :], preferred_element_type=jnp.float32
        )

    def to_mate(k, step):
        copies1[k, step] = remote(
            parts[k].at[step, pl.ds(pl.multiple_of((1 - core) * rows, rows), rows)],
            first[k].at[step], send1.at[k, step], recv1.at[k, step], tok, mate,
        )
        copies1[k, step].start()

    def onward(k, step):
        copies1[k, step].wait_recv()
        own = parts[k][step, pl.ds(pl.multiple_of(core * rows, rows), rows), :]
        held[k][step] = own + first[k][step]
        if step:
            copies2[k, step] = remote(
                held[k].at[step], second[k].at[step], send2.at[k, step], recv2.at[k, step],
                tok, ((pair + step) % chips) * 2 + core,
            )
            copies2[k, step].start()

    waiting = []
    for number, step in enumerate(order):
        for k in range(2):
            if number == 0:
                loads[k].wait()
            loads[k, step].wait()
            depth = lhs[k].shape[2]
            cut = depth // 2 if k else depth
            parts[k][step] = project(k, step, 0, cut)
            for item in waiting:
                onward(*item)
            waiting = []
            if cut < depth:
                parts[k][step] += project(k, step, cut, depth)
            to_mate(k, step)
            waiting = [(k, step)]
    for item in waiting:
        onward(*item)
    for k in range(2):
        total = held[k][0]
        for step in range(1, chips):
            copies2[k, step].wait_recv()
            total += second[k][step]
        outs[k][...] = total
    for copy in trades:
        copy.wait_recv()
    for copy in trades + list(copies1.values()) + list(copies2.values()):
        copy.wait_send()


def grads_kernel(sizes, part, slots, stored_rows, *refs):
    feats, group_toks, groups, local, rows, spacing, pieces, early = sizes
    total, out = refs[early : early + 2]
    recv, grads, heads, picked, scored, landed, late = refs[early + 2 : early + 9]
    sends, recvs, gsend, grecv, hsend, hrecv, psend, precv, ssend, srecv, lsend, lrecv = refs[
        early + 9 :
    ]
    highest = lax.Precision.HIGHEST
    near, count, height, rank = part.shape
    held = group_toks * local
    tall = height // pieces
    tok, feat = lax.axis_index("tok"), lax.axis_index("feat")
    group, spot = tok // group_toks, tok % group_toks
    me = spot * feats + feat

    def place(step):
        peer = (me + step) % count
        return peer // feats, peer % feats

    barrier = pltpu.get_barrier_semaphore()
    for step in range(1, count):
        peer_spot, peer_feat = place(step)
        greet(barrier, group * group_toks + peer_spot, peer_feat)

    @pl.when(group > 0)
    def _():
        greet(barrier, tok - group_toks, feat)

    @pl.when(group < groups - 1)
    def _():
        greet(barrier, tok + group_toks, feat)

    ends = (group > 0).astype(jnp.int32) + (group < groups - 1).astype(jnp.int32)
    pl.semaphore_wait(barrier, count - 1 + ends)

    copies = {}
    for piece in range(pieces):
        lines = pl.ds(piece * tall, tall)
        for step in range(1, count):
            peer_spot, peer_feat = place(step)
            copies[piece, step] = remote(
                part.at[:, peer_feat * group_toks + peer_spot, lines, :],
                recv.at[step, :, lines, :],
                sends.at[piece, step], recvs.at[piece, step],
                group * group_toks + peer_spot, peer_feat,
            )
            copies[piece, step].start()
    recv[0] = part[:, feat * group_toks + spot]
    width = late.shape[2]
    kept = pltpu.make_async_copy(
        stored_rows.at[:, pl.ds(pl.multiple_of(spot * width, width), width)], late.at[0], lsend.at[0]
    )
    kept.start()
    trades = []
    for step in range(early + 1, group_toks):
        to = (spot + step) % group_toks
        trades.append(remote(
            stored_rows.at[:, pl.ds(pl.multiple_of(to * width, width), width)],
            late.at[step - early], lsend.at[step - early], lrecv.at[step - early],
            group * group_toks + to, feat,
        ))
        trades[-1].start()
    stored = [late.at[0], *refs[:early]] + [
        late.at[step - early] for step in range(early + 1, group_toks)
    ]

    terms = {}
    for source in range(count):
        base = (source // feats) * local + ((source % feats) * rows) // spacing
        for k in range(near):
            terms.setdefault(base + k, []).append((source, k))

    def block(at, piece):
        return grads.at[
            pl.ds(piece * tall, tall), pl.ds(pl.multiple_of(at * held, held), held), :
        ]

    def move(way, step, piece):
        at = jnp.clip(group - step if way == 0 else group + step, 0, groups - 1)
        to = tok + group_toks if way == 0 else tok - group_toks
        head = heads.at[at, pl.ds(piece * tall, tall), :]
        index = way, step, piece
        return (
            remote(block(at, piece), block(at, piece), gsend.at[index], grecv.at[index], to, feat),
            remote(head, head, hsend.at[index], hrecv.at[index], to, feat),
        )

    def each(way, step, piece, what, when):
        @pl.when(when)
        def _():
            for copy in move(way, step, piece):
                getattr(copy, what)()

    def sending(way, step):
        if way == 0:
            return (group - step >= 0) & (group + 1 < groups)
        return (group + step < groups) & (group - 1 >= 0)

    def taking(way, step):
        return group - 1 - step >= 0 if way == 0 else group + 1 + step < groups

    for piece in range(pieces):
        lines = pl.ds(piece * tall, tall)
        for step in range(1, count):
            copies[piece, step].wait_recv()
        for row in range(held + 1):
            value = None
            for source, k in terms.get(row, []):
                term = recv[(me + count - source) % count, k, lines, :]
                value = term if value is None else value + term
            if row == 0:
                heads[group, lines, :] = value
            else:
                block(group, piece)[:, row - 1, :] = value
        for way in range(2):
            if groups > 1:
                each(way, 0, piece, "start", sending(way, 0))
    seqs = grads.shape[1]
    row = lax.broadcasted_iota(jnp.int32, (held, seqs), 0) + group * held
    pick = jnp.where(slots[...] == row, 1.0, 0.0).astype(jnp.float32)
    wide = height * rank
    part_wide = tall * rank
    first_lane = pl.multiple_of(spot * wide, wide)
    score = jnp.zeros((group_toks * late.shape[1], seqs), jnp.float32)

    def finish(piece, score):
        lines = range(piece * tall, (piece + 1) * tall)
        for at in range(1, groups):
            span = pl.ds(piece * tall, tall)
            grads[span, at * held - 1, :] += heads[at, span, :]
        for line in lines:
            lane = pl.ds(line * rank, rank)
            taken = jnp.dot(
                pick, grads[line], precision=highest, preferred_element_type=jnp.float32
            )
            for q in range(group_toks):
                picked[q, :, lane] = taken[q * local : (q + 1) * local]
        lanes = pl.ds(piece * part_wide, part_wide)
        mine = pl.ds(pl.multiple_of(first_lane + piece * part_wide, part_wide), part_wide)
        for step in range(1, group_toks):
            to = (spot + step) % group_toks
            trades.append(remote(
                picked.at[to, :, lanes], out.at[:, mine],
                psend.at[piece, step], precv.at[piece, step],
                group * group_toks + to, feat,
            ))
            trades[-1].start()
        out[:, mine] = picked[spot, :, lanes]
        if piece == 0:
            kept.wait()
            for copy in trades[: group_toks - 1 - early]:
                copy.wait_recv()
        for line in lines:
            lane = pl.ds(line * rank, rank)
            block_rows = jnp.concatenate([ref[:, lane] for ref in stored], axis=0)
            score += lax.dot_general(
                block_rows, grads[line], (((1,), (1,)), ((), ())),
                precision=highest, preferred_element_type=jnp.float32,
            )
        return score

    for step in range(max(groups - 1, 1)):
        for piece in range(pieces):
            if groups > 1:
                for way in range(2):
                    each(way, step, piece, "wait_recv", taking(way, step))
                    if step + 1 < groups - 1:
                        each(way, step + 1, piece, "start", sending(way, step + 1))
            if step >= groups - 2:
                for way in range(2):
                    for sent in range(groups - 1):
                        each(way, sent, piece, "wait_send", sending(way, sent))
                score = finish(piece, score)

    scored[...] = jnp.zeros_like(scored)
    few = scored.shape[2]
    for step in range(group_toks):
        for f in range(feats):
            first = (step * feats + f) * few
            scored[step, f, :, : score.shape[1]] = score[first : first + few]
    parts = []
    for step in range(group_toks):
        for turn in range(feats):
            if step or turn:
                to = (feat + turn) % feats
                parts.append(remote(
                    scored.at[step, to], landed.at[step, turn],
                    ssend.at[step, turn], srecv.at[step, turn],
                    group * group_toks + (spot + group_toks - step) % group_toks, to,
                ))
                parts[-1].start()
    summed = scored[0, feat]
    for number, copy in enumerate(parts, 1):
        copy.wait_recv()
        summed += landed[number // feats, number % feats]
    column = lax.broadcasted_iota(jnp.int32, (seqs, seqs), 0)
    by_slot = jnp.where(slots[...] == column, 1.0, 0.0).astype(jnp.float32)
    total[...] = lax.dot_general(
        summed[:, :seqs], by_slot, (((1,), (1,)), ((), ())),
        precision=highest, preferred_element_type=jnp.float32,
    )
    for copy in trades[group_toks - 1 - early :]:
        copy.wait_recv()
    for copy in trades + parts + list(copies.values()):
        copy.wait_send()


def body(
    activations,
    out_grads,
    proj_in,
    proj_out,
    left_factor,
    right_factor,
    seq_lengths,
    seq_slots,
    stored_grads,
):
    highest = lax.Precision.HIGHEST
    f32 = jnp.float32
    dma = pltpu.SemaphoreType.DMA
    feats, toks = lax.axis_size("feat"), lax.axis_size("tok")
    group_toks = 4 if toks % 4 == 0 else 1
    chips, groups, count = feats // 2, toks // group_toks, group_toks * feats
    rank = right_factor.shape[0]
    tok_rows = activations.shape[0]
    seq_count = seq_lengths.shape[0]
    local = seq_count // toks
    spacing = tok_rows // local
    rows = tok_rows // feats
    height = rank // count
    near = max(rows // spacing, 1) + 1
    feat, tok = lax.axis_index("feat"), lax.axis_index("tok")
    spot = tok % group_toks
    store_rows, width = stored_grads.shape
    wide = width // group_toks

    early = group_toks - 1
    any_space = pl.BlockSpec(memory_space=pl.ANY)
    lefts, mats = (out_grads, activations), (proj_out, proj_in)
    pair_rows = pltpu.VMEM((chips, rows, rank), f32)
    out_total, in_total, *traded = pl.pallas_call(
        functools.partial(project_kernel, (chips, rows, group_toks, early)),
        out_shape=[jax.ShapeDtypeStruct((rows, rank), f32)] * 2
        + [jax.ShapeDtypeStruct((store_rows, wide), f32)] * early,
        in_specs=[any_space] * 5,
        out_specs=[VMEM] * (2 + early),
        scratch_shapes=[pltpu.VMEM((chips, 2 * rows, m.shape[1]), m.dtype) for m in lefts]
        + [pltpu.VMEM(m.shape, m.dtype) for m in mats]
        + [pltpu.VMEM((chips, 2 * rows, rank), f32)] * 2
        + [pair_rows] * 6
        + [dma((2, chips + 1))]
        + [dma((2, chips))] * 4
        + [dma((early,))] * 2,
        compiler_params=pltpu.CompilerParams(
            collective_id=0, has_side_effects=True, vmem_limit_bytes=60 << 20
        ),
        name="project",
    )(*lefts, *mats, stored_grads)
    right_side = jnp.dot(in_total, right_factor, precision=highest)
    left_side = jnp.dot(out_total, left_factor.T, precision=highest)

    places = tok * tok_rows + feat * rows + jnp.arange(rows, dtype=jnp.int32)
    numbers = jnp.arange(seq_count, dtype=jnp.int32)
    close = tok * local + (feat * rows) // spacing - 1 + jnp.arange(near, dtype=jnp.int32)
    starts = jnp.sum(jnp.where(numbers[None, :] < close[:, None], seq_lengths[None, :], 0), axis=1)
    sizes = jnp.sum(jnp.where(numbers[None, :] == close[:, None], seq_lengths[None, :], 0), axis=1)
    inside = (places[:, None] >= starts[None, :]) & (places[:, None] < (starts + sizes)[None, :])
    weights = inside.astype(f32) / jnp.maximum(sizes, 1).astype(f32)[None, :]
    spread = jnp.concatenate([weights[:, k : k + 1] * left_side for k in range(near)], axis=1)
    part = lax.dot_general(spread, right_side, (((0,), (0,)), ((), ())), precision=highest)

    score_rows = store_rows // feats
    lanes = seq_count + -seq_count % 128
    pieces = 2 if height % 16 == 0 else 1
    hops = max(groups - 1, 1)
    sizes_ = (feats, group_toks, groups, local, rows, spacing, pieces, early)
    scores, own_rows = pl.pallas_call(
        functools.partial(grads_kernel, sizes_),
        out_shape=[
            jax.ShapeDtypeStruct((score_rows, seq_count), f32),
            jax.ShapeDtypeStruct((local, width), f32),
        ],
        in_specs=[VMEM] * 2 + [any_space] + [VMEM] * early,
        out_specs=[VMEM] * 2,
        scratch_shapes=[
            pltpu.VMEM((count, near, height, rank), f32),
            pltpu.VMEM((height, seq_count, rank), f32),
            pltpu.VMEM((groups, height, rank), f32),
            pltpu.VMEM((group_toks, local, wide), f32),
            pltpu.VMEM((group_toks, feats, score_rows, lanes), f32),
            pltpu.VMEM((group_toks, feats, score_rows, lanes), f32),
            pltpu.VMEM((group_toks - early, store_rows, wide), f32),
        ]
        + [dma((pieces, count))] * 2
        + [dma((2, hops, pieces))] * 4
        + [dma((pieces, group_toks))] * 2
        + [dma((group_toks, feats))] * 2
        + [dma((group_toks - early,))] * 2,
        compiler_params=pltpu.CompilerParams(collective_id=1, has_side_effects=True),
        name="grads",
    )(part.reshape(near, count, height, rank), seq_slots.reshape(1, seq_count), stored_grads, *traded)
    return scores, own_rows


def solution(mesh):
    placed = (
        P("tok", "feat"),
        P("tok", "feat"),
        P("feat", None),
        P("feat", None),
        P(),
        P(),
        P(),
        P(),
        P("tok", "feat"),
    )
    return jax.shard_map(
        body,
        mesh=mesh,
        in_specs=placed,
        out_specs=(P(("tok", "feat"), None), P("tok", "feat")),
        check_vma=False,
    )
```

```python
import functools

import jax
import jax.numpy as jnp
from jax import lax
from jax.experimental import pallas as pl
from jax.experimental.pallas import tpu as pltpu
from jax.sharding import PartitionSpec as P

MESH = pl.DeviceIdType.MESH
VMEM = pl.BlockSpec(memory_space=pltpu.VMEM)


def remote(src, dst, send_sem, recv_sem, tok, feat):
    return pltpu.make_async_remote_copy(
        src_ref=src, dst_ref=dst, send_sem=send_sem, recv_sem=recv_sem,
        device_id=(tok, feat), device_id_type=MESH,
    )


def greet(barrier, tok, feat):
    pl.semaphore_signal(barrier, inc=1, device_id=(tok, feat), device_id_type=MESH)


def project_kernel(sizes, *refs):
    chips, rows, group_toks, early = sizes
    rows_in, mats_in, stored = refs[0:2], refs[2:4], refs[4]
    outs, traded = refs[5:7], refs[7 : 7 + early]
    refs = refs[7 + early :]
    lhs, rhs, parts, first, held, second = (refs[2 * n : 2 * n + 2] for n in range(6))
    load, send1, recv1, send2, recv2, tsend, trecv = refs[12:]
    tok, feat = lax.axis_index("tok"), lax.axis_index("feat")
    spot = tok % group_toks
    pair, core = feat // 2, feat % 2
    mate = pair * 2 + (1 - core)
    both = 2 * rows
    order = list(range(1, chips)) + [0]

    def lines(step):
        return pl.ds(pl.multiple_of(((pair + step) % chips) * both, both), both)

    loads = {}
    for step in order:
        for k in range(2):
            if step == order[0]:
                loads[k] = pltpu.make_async_copy(mats_in[k], rhs[k], load.at[k, chips])
                loads[k].start()
            loads[k, step] = pltpu.make_async_copy(
                rows_in[k].at[lines(step)], lhs[k].at[step], load.at[k, step]
            )
            loads[k, step].start()

    barrier = pltpu.get_barrier_semaphore()
    greet(barrier, tok, mate)
    for step in range(1, chips):
        greet(barrier, tok, ((pair + step) % chips) * 2 + core)
    for step in range(1, group_toks):
        greet(barrier, tok - spot + (spot + step) % group_toks, feat)
    pl.semaphore_wait(barrier, chips + group_toks - 1)

    wide = traded[0].shape[1]
    trades = []
    for step in range(1, early + 1):
        to = (spot + step) % group_toks
        trades.append(remote(
            stored.at[:, pl.ds(pl.multiple_of(to * wide, wide), wide)], traded[step - 1],
            tsend.at[step - 1], trecv.at[step - 1], tok - spot + to, feat,
        ))
        trades[-1].start()

    copies1, copies2 = {}, {}

    def project(k, step, low, high):
        return jnp.dot(
            lhs[k][step, :, low:high], rhs[k][low:high, :], preferred_element_type=jnp.float32
        )

    def to_mate(k, step):
        copies1[k, step] = remote(
            parts[k].at[step, pl.ds(pl.multiple_of((1 - core) * rows, rows), rows)],
            first[k].at[step], send1.at[k, step], recv1.at[k, step], tok, mate,
        )
        copies1[k, step].start()

    def onward(k, step):
        copies1[k, step].wait_recv()
        own = parts[k][step, pl.ds(pl.multiple_of(core * rows, rows), rows), :]
        held[k][step] = own + first[k][step]
        if step:
            copies2[k, step] = remote(
                held[k].at[step], second[k].at[step], send2.at[k, step], recv2.at[k, step],
                tok, ((pair + step) % chips) * 2 + core,
            )
            copies2[k, step].start()

    waiting = []
    for number, step in enumerate(order):
        for k in range(2):
            if number == 0:
                loads[k].wait()
            loads[k, step].wait()
            depth = lhs[k].shape[2]
            cut = depth // 2 if k else depth
            parts[k][step] = project(k, step, 0, cut)
            for item in waiting:
                onward(*item)
            waiting = []
            if cut < depth:
                parts[k][step] += project(k, step, cut, depth)
            to_mate(k, step)
            waiting = [(k, step)]
    for item in waiting:
        onward(*item)
    for k in range(2):
        total = held[k][0]
        for step in range(1, chips):
            copies2[k, step].wait_recv()
            total += second[k][step]
        outs[k][...] = total
    for copy in trades:
        copy.wait_recv()
    for copy in trades + list(copies1.values()) + list(copies2.values()):
        copy.wait_send()


def grads_kernel(sizes, part, slots, stored_rows, *refs):
    feats, group_toks, groups, local, rows, spacing, pieces, early = sizes
    total, out = refs[early : early + 2]
    recv, grads, heads, picked, scored, landed, late = refs[early + 2 : early + 9]
    sends, recvs, gsend, grecv, hsend, hrecv, psend, precv, ssend, srecv, lsend, lrecv = refs[
        early + 9 :
    ]
    highest = lax.Precision.HIGHEST
    near, count, height, rank = part.shape
    held = group_toks * local
    tall = height // pieces
    tok, feat = lax.axis_index("tok"), lax.axis_index("feat")
    group, spot = tok // group_toks, tok % group_toks
    me = spot * feats + feat

    def place(step):
        peer = (me + step) % count
        return peer // feats, peer % feats

    barrier = pltpu.get_barrier_semaphore()
    for step in range(1, count):
        peer_spot, peer_feat = place(step)
        greet(barrier, group * group_toks + peer_spot, peer_feat)

    @pl.when(group > 0)
    def _():
        greet(barrier, tok - group_toks, feat)

    @pl.when(group < groups - 1)
    def _():
        greet(barrier, tok + group_toks, feat)

    ends = (group > 0).astype(jnp.int32) + (group < groups - 1).astype(jnp.int32)
    pl.semaphore_wait(barrier, count - 1 + ends)

    copies = {}
    for piece in range(pieces):
        lines = pl.ds(piece * tall, tall)
        for step in range(1, count):
            peer_spot, peer_feat = place(step)
            copies[piece, step] = remote(
                part.at[:, peer_feat * group_toks + peer_spot, lines, :],
                recv.at[step, :, lines, :],
                sends.at[piece, step], recvs.at[piece, step],
                group * group_toks + peer_spot, peer_feat,
            )
            copies[piece, step].start()
    recv[0] = part[:, feat * group_toks + spot]
    width = late.shape[2]
    kept = pltpu.make_async_copy(
        stored_rows.at[:, pl.ds(pl.multiple_of(spot * width, width), width)], late.at[0], lsend.at[0]
    )
    kept.start()
    trades = []
    stored = [late.at[0], *refs[:early]] + [
        late.at[step - early] for step in range(early + 1, group_toks)
    ]

    terms = {}
    for source in range(count):
        base = (source // feats) * local + ((source % feats) * rows) // spacing
        for k in range(near):
            terms.setdefault(base + k, []).append((source, k))

    def block(at, piece):
        return grads.at[
            pl.ds(piece * tall, tall), pl.ds(pl.multiple_of(at * held, held), held), :
        ]

    def move(way, step, piece):
        at = jnp.clip(group - step if way == 0 else group + step, 0, groups - 1)
        to = tok + group_toks if way == 0 else tok - group_toks
        head = heads.at[at, pl.ds(piece * tall, tall), :]
        index = way, step, piece
        return (
            remote(block(at, piece), block(at, piece), gsend.at[index], grecv.at[index], to, feat),
            remote(head, head, hsend.at[index], hrecv.at[index], to, feat),
        )

    def each(way, step, piece, what, when):
        @pl.when(when)
        def _():
            for copy in move(way, step, piece):
                getattr(copy, what)()

    def sending(way, step):
        if way == 0:
            return (group - step >= 0) & (group + 1 < groups)
        return (group + step < groups) & (group - 1 >= 0)

    def taking(way, step):
        return group - 1 - step >= 0 if way == 0 else group + 1 + step < groups

    for piece in range(pieces):
        lines = pl.ds(piece * tall, tall)
        for step in range(1, count):
            copies[piece, step].wait_recv()
        for row in range(held + 1):
            value = None
            for source, k in terms.get(row, []):
                term = recv[(me + count - source) % count, k, lines, :]
                value = term if value is None else value + term
            if row == 0:
                heads[group, lines, :] = value
            else:
                block(group, piece)[:, row - 1, :] = value
        for way in range(2):
            if groups > 1:
                each(way, 0, piece, "start", sending(way, 0))
    for step in range(early + 1, group_toks):
        to = (spot + step) % group_toks
        trades.append(remote(
            stored_rows.at[:, pl.ds(pl.multiple_of(to * width, width), width)],
            late.at[step - early], lsend.at[step - early], lrecv.at[step - early],
            group * group_toks + to, feat,
        ))
        trades[-1].start()
    seqs = grads.shape[1]
    row = lax.broadcasted_iota(jnp.int32, (held, seqs), 0) + group * held
    pick = jnp.where(slots[...] == row, 1.0, 0.0).astype(jnp.float32)
    wide = height * rank
    part_wide = tall * rank
    first_lane = pl.multiple_of(spot * wide, wide)
    score = jnp.zeros((group_toks * late.shape[1], seqs), jnp.float32)

    def finish(piece, score):
        lines = range(piece * tall, (piece + 1) * tall)
        for at in range(1, groups):
            span = pl.ds(piece * tall, tall)
            grads[span, at * held - 1, :] += heads[at, span, :]
        for line in lines:
            lane = pl.ds(line * rank, rank)
            taken = jnp.dot(
                pick, grads[line], precision=highest, preferred_element_type=jnp.float32
            )
            for q in range(group_toks):
                picked[q, :, lane] = taken[q * local : (q + 1) * local]
        lanes = pl.ds(piece * part_wide, part_wide)
        mine = pl.ds(pl.multiple_of(first_lane + piece * part_wide, part_wide), part_wide)
        for step in range(1, group_toks):
            to = (spot + step) % group_toks
            trades.append(remote(
                picked.at[to, :, lanes], out.at[:, mine],
                psend.at[piece, step], precv.at[piece, step],
                group * group_toks + to, feat,
            ))
            trades[-1].start()
        out[:, mine] = picked[spot, :, lanes]
        if piece == 0:
            kept.wait()
            for copy in trades[: group_toks - 1 - early]:
                copy.wait_recv()
        for line in lines:
            lane = pl.ds(line * rank, rank)
            block_rows = jnp.concatenate([ref[:, lane] for ref in stored], axis=0)
            score += lax.dot_general(
                block_rows, grads[line], (((1,), (1,)), ((), ())),
                precision=highest, preferred_element_type=jnp.float32,
            )
        return score

    for step in range(max(groups - 1, 1)):
        for piece in range(pieces):
            if groups > 1:
                for way in range(2):
                    each(way, step, piece, "wait_recv", taking(way, step))
                    if step + 1 < groups - 1:
                        each(way, step + 1, piece, "start", sending(way, step + 1))
            if step >= groups - 2:
                for way in range(2):
                    for sent in range(groups - 1):
                        each(way, sent, piece, "wait_send", sending(way, sent))
                score = finish(piece, score)

    scored[...] = jnp.zeros_like(scored)
    few = scored.shape[2]
    for step in range(group_toks):
        for f in range(feats):
            first = (step * feats + f) * few
            scored[step, f, :, : score.shape[1]] = score[first : first + few]
    parts = []
    for step in range(group_toks):
        for turn in range(feats):
            if step or turn:
                to = (feat + turn) % feats
                parts.append(remote(
                    scored.at[step, to], landed.at[step, turn],
                    ssend.at[step, turn], srecv.at[step, turn],
                    group * group_toks + (spot + group_toks - step) % group_toks, to,
                ))
                parts[-1].start()
    summed = scored[0, feat]
    for number, copy in enumerate(parts, 1):
        copy.wait_recv()
        summed += landed[number // feats, number % feats]
    column = lax.broadcasted_iota(jnp.int32, (seqs, seqs), 0)
    by_slot = jnp.where(slots[...] == column, 1.0, 0.0).astype(jnp.float32)
    total[...] = lax.dot_general(
        summed[:, :seqs], by_slot, (((1,), (1,)), ((), ())),
        precision=highest, preferred_element_type=jnp.float32,
    )
    for copy in trades[group_toks - 1 - early :]:
        copy.wait_recv()
    for copy in trades + parts + list(copies.values()):
        copy.wait_send()


def body(
    activations,
    out_grads,
    proj_in,
    proj_out,
    left_factor,
    right_factor,
    seq_lengths,
    seq_slots,
    stored_grads,
):
    highest = lax.Precision.HIGHEST
    f32 = jnp.float32
    dma = pltpu.SemaphoreType.DMA
    feats, toks = lax.axis_size("feat"), lax.axis_size("tok")
    group_toks = 4 if toks % 4 == 0 else 1
    chips, groups, count = feats // 2, toks // group_toks, group_toks * feats
    rank = right_factor.shape[0]
    tok_rows = activations.shape[0]
    seq_count = seq_lengths.shape[0]
    local = seq_count // toks
    spacing = tok_rows // local
    rows = tok_rows // feats
    height = rank // count
    near = max(rows // spacing, 1) + 1
    feat, tok = lax.axis_index("feat"), lax.axis_index("tok")
    spot = tok % group_toks
    store_rows, width = stored_grads.shape
    wide = width // group_toks

    early = group_toks - 2
    any_space = pl.BlockSpec(memory_space=pl.ANY)
    lefts, mats = (out_grads, activations), (proj_out, proj_in)
    pair_rows = pltpu.VMEM((chips, rows, rank), f32)
    out_total, in_total, *traded = pl.pallas_call(
        functools.partial(project_kernel, (chips, rows, group_toks, early)),
        out_shape=[jax.ShapeDtypeStruct((rows, rank), f32)] * 2
        + [jax.ShapeDtypeStruct((store_rows, wide), f32)] * early,
        in_specs=[any_space] * 5,
        out_specs=[VMEM] * (2 + early),
        scratch_shapes=[pltpu.VMEM((chips, 2 * rows, m.shape[1]), m.dtype) for m in lefts]
        + [pltpu.VMEM(m.shape, m.dtype) for m in mats]
        + [pltpu.VMEM((chips, 2 * rows, rank), f32)] * 2
        + [pair_rows] * 6
        + [dma((2, chips + 1))]
        + [dma((2, chips))] * 4
        + [dma((early,))] * 2,
        compiler_params=pltpu.CompilerParams(
            collective_id=0, has_side_effects=True, vmem_limit_bytes=60 << 20
        ),
        name="project",
    )(*lefts, *mats, stored_grads)
    right_side = jnp.dot(in_total, right_factor, precision=highest)
    left_side = jnp.dot(out_total, left_factor.T, precision=highest)

    places = tok * tok_rows + feat * rows + jnp.arange(rows, dtype=jnp.int32)
    numbers = jnp.arange(seq_count, dtype=jnp.int32)
    close = tok * local + (feat * rows) // spacing - 1 + jnp.arange(near, dtype=jnp.int32)
    starts = jnp.sum(jnp.where(numbers[None, :] < close[:, None], seq_lengths[None, :], 0), axis=1)
    sizes = jnp.sum(jnp.where(numbers[None, :] == close[:, None], seq_lengths[None, :], 0), axis=1)
    inside = (places[:, None] >= starts[None, :]) & (places[:, None] < (starts + sizes)[None, :])
    weights = inside.astype(f32) / jnp.maximum(sizes, 1).astype(f32)[None, :]
    spread = jnp.concatenate([weights[:, k : k + 1] * left_side for k in range(near)], axis=1)
    part = lax.dot_general(spread, right_side, (((0,), (0,)), ((), ())), precision=highest)

    score_rows = store_rows // feats
    lanes = seq_count + -seq_count % 128
    pieces = 2 if height % 16 == 0 else 1
    hops = max(groups - 1, 1)
    sizes_ = (feats, group_toks, groups, local, rows, spacing, pieces, early)
    scores, own_rows = pl.pallas_call(
        functools.partial(grads_kernel, sizes_),
        out_shape=[
            jax.ShapeDtypeStruct((score_rows, seq_count), f32),
            jax.ShapeDtypeStruct((local, width), f32),
        ],
        in_specs=[VMEM] * 2 + [any_space] + [VMEM] * early,
        out_specs=[VMEM] * 2,
        scratch_shapes=[
            pltpu.VMEM((count, near, height, rank), f32),
            pltpu.VMEM((height, seq_count, rank), f32),
            pltpu.VMEM((groups, height, rank), f32),
            pltpu.VMEM((group_toks, local, wide), f32),
            pltpu.VMEM((group_toks, feats, score_rows, lanes), f32),
            pltpu.VMEM((group_toks, feats, score_rows, lanes), f32),
            pltpu.VMEM((group_toks - early, store_rows, wide), f32),
        ]
        + [dma((pieces, count))] * 2
        + [dma((2, hops, pieces))] * 4
        + [dma((pieces, group_toks))] * 2
        + [dma((group_toks, feats))] * 2
        + [dma((group_toks - early,))] * 2,
        compiler_params=pltpu.CompilerParams(collective_id=1, has_side_effects=True),
        name="grads",
    )(part.reshape(near, count, height, rank), seq_slots.reshape(1, seq_count), stored_grads, *traded)
    return scores, own_rows


def solution(mesh):
    placed = (
        P("tok", "feat"),
        P("tok", "feat"),
        P("feat", None),
        P("feat", None),
        P(),
        P(),
        P(),
        P(),
        P("tok", "feat"),
    )
    return jax.shard_map(
        body,
        mesh=mesh,
        in_specs=placed,
        out_specs=(P(("tok", "feat"), None), P("tok", "feat")),
        check_vma=False,
    )
```
